32 devices in a mesh: grp: 4 (over z), dev: 8 (over y, x, core).
Axes of the slice: x: 2, y: 2, z: 4, core: 2. Of those that a mesh axis runs over, the one named last changes fastest.
Arguments:
- matrix: float32 [65536, 1024], P(('grp', 'dev')), may hold values from -60 to 60
- block_order: int32 [4, 128], P('grp'), may hold values from 0 to 127, as said below
- counts: int32 [4, 8], P('grp'), may hold values from 0 to 32, as said below
- sign_bits: int32 [4, 128, 128], P('grp'), may hold values from 0 to 1
- row_mask: int32 [4, 128, 128], P('grp'), may hold values from 0 to 1, as said below
Outputs:
- sketch: float32 [32768, 1024], P(('grp', 'dev'))
- group_factor: float32 [4, 1024, 1024], P('grp', 'dev')
- factor: float32 [1024, 1024], P('dev')
The draws below stay inside these ranges and needn't reach their ends.
Inputs may be any that keep to these rules, and one draw needn't show every extreme that they name: Each row of block_order is a permutation of the group's block indices; at most 4 blocks of one device's blocks are placed in the positions held by one device, and some pair reaches 4. `counts`: each row sums to 128; its largest entry is exactly 32. `row_mask`: exactly 32 ones in each row of 128.
All inputs are finite; a program needn't handle non-finite values.
Results may differ from the reference program's by a relative error of at most 0.0003.
Values sent between devices are 32-bit elements; how exact they have to be, the bound alone decides.
No kernel may reach another device: no remote copies, remote signals or barrier semaphores. Data moves between devices by JAX's collectives and lax.ppermute only.
A program may use at most 128 MiB of HBM per device.

```python
import math
import jax
import jax.numpy as jnp
from jax import lax

COLS = 1024
BLOCK = 128
KEEP = 32
BLOCKS_DEV = 16
POSITIONS = 128
MOST = 32
ROWS = 65536
N_GRP = 4
N_DEV = 8


def layout_group(key):
    keys = jax.random.split(key, 5)
    positions = N_DEV * BLOCKS_DEV
    device_order = jax.random.permutation(keys[0], N_DEV).astype(jnp.int32)
    smaller = jax.random.randint(keys[1], (N_DEV // 2,), 0, BLOCKS_DEV + 1).astype(jnp.int32)
    smaller = smaller.at[0].set(0)
    count_row = jnp.zeros((N_DEV,), jnp.int32)
    count_row = count_row.at[device_order[0::2]].set(2 * BLOCKS_DEV - smaller)
    count_row = count_row.at[device_order[1::2]].set(smaller)
    run_ends = jnp.cumsum(count_row)
    block_locations = jnp.arange(positions, dtype=jnp.int32)
    owners = jnp.sum((block_locations[:, None] >= run_ends[None, :]).astype(jnp.int32), axis=1)
    relabel = jax.random.permutation(keys[2], N_DEV).astype(jnp.int32)
    source = relabel[block_locations % N_DEV]
    noise_one = jax.random.randint(keys[3], (positions,), 0, positions).astype(jnp.int32)
    within = jnp.argsort(owners * (positions * positions) + noise_one * positions + block_locations)
    source = source[within]
    noise_two = jax.random.randint(keys[4], (positions,), 0, positions).astype(jnp.int32)
    by_source = jnp.argsort(source * (positions * positions) + noise_two * positions + block_locations)
    ranks = jnp.zeros((positions,), jnp.int32).at[by_source].set(block_locations - source[by_source] * BLOCKS_DEV)
    return (source * BLOCKS_DEV + ranks, count_row)


def full_arrangement(key):
    group_keys = jax.random.split(jax.random.fold_in(key, 7), N_GRP)
    return jax.vmap(layout_group)(group_keys)


def draw_block_order(key, part):
    return full_arrangement(key)[0].astype(jnp.int32)


def draw_counts(key, part):
    return full_arrangement(key)[1].astype(jnp.int32)


def draw_row_mask(key, part):
    scores = jax.random.randint(key, (N_GRP, POSITIONS, BLOCK), 0, 2 ** 20).astype(jnp.int32)
    scores = scores * BLOCK + jnp.arange(BLOCK, dtype=jnp.int32)[None, None, :]
    ranks = jnp.argsort(jnp.argsort(scores, axis=2), axis=2)
    return (ranks < KEEP).astype(jnp.int32)


def draw_matrix(key, part):
    keys = jax.random.split(key, 3)
    col_scale = jnp.exp(jax.random.uniform(keys[2], (1, COLS), jnp.float32, math.log(0.3), math.log(3.0)))
    base = jnp.clip(jax.random.normal(keys[0], (ROWS, COLS), jnp.float32), -5.0, 5.0)
    row_scale = jnp.exp(jax.random.uniform(keys[1], (ROWS, 1), jnp.float32, math.log(0.3), math.log(3.0)))
    return (base * row_scale * col_scale).astype(jnp.float32)


def set_ends(array, rng, smallest, largest):
    longest = array.shape.index(max(array.shape))
    spots = []
    for shift in (0, 1):
        where = [jax.random.randint(jax.random.fold_in(rng, axis), (), 0, length) for axis, length in enumerate(array.shape)]
        where[longest] = (where[longest] + shift) % array.shape[longest]
        spots.append(tuple(where))
    return array.at[spots[0]].set(smallest).at[spots[1]].set(largest)


def setup_inputs(seed: int = 0) -> dict:
    streams_of = jax.random.split(jax.random.key(seed), 6)
    return {
        "matrix": draw_matrix(jax.random.fold_in(streams_of[5], 71), 0),
        "block_order": draw_block_order(jax.random.fold_in(streams_of[5], 71), 0),
        "counts": draw_counts(jax.random.fold_in(streams_of[5], 71), 0),
        "sign_bits": set_ends(jax.random.randint(streams_of[3], (N_GRP, POSITIONS, BLOCK), 0, 2), jax.random.fold_in(streams_of[3], 1), 0, 1).astype(jnp.int32),
        "row_mask": draw_row_mask(jax.random.fold_in(streams_of[5], 71), 0),
    }


def hadamard(order_of):
    indices = jnp.arange(order_of, dtype=jnp.int32)
    common = jnp.bitwise_and(indices[:, None], indices[None, :])
    parity = jnp.zeros_like(common)
    for shift_by in range(order_of.bit_length() - 1):
        parity = parity + jnp.bitwise_and(jnp.right_shift(common, shift_by), 1)
    return (1 - 2 * (parity % 2)).astype(jnp.float32)

def mix_blocks(block_list, mask_rows, sign_rows, walsh_sign_matrix):
    running = jnp.cumsum(mask_rows, axis=1) - 1
    choose_row = jnp.arange(KEEP, dtype=jnp.int32)[None, :, None]
    select_rows = ((mask_rows[:, None, :] == 1) & (running[:, None, :] == choose_row)).astype(jnp.float32)
    mixing_transform = jnp.einsum('jlf,fp->jlp', select_rows, walsh_sign_matrix, precision=lax.Precision.HIGHEST)
    mixing_transform = mixing_transform * (1 - 2 * sign_rows).astype(jnp.float32)[:, None, :]
    normalize_rows = float(walsh_sign_matrix.shape[0]) ** (-0.5)
    return jnp.einsum('uwd,udk->uwk', mixing_transform, block_list, precision=lax.Precision.HIGHEST) * normalize_rows

def reference(matrix, block_order, counts, sign_bits, row_mask):
    walsh_sign_matrix = hadamard(BLOCK)

    def one_group(group_id):
        group_rows = lax.dynamic_slice_in_dim(matrix, group_id * (POSITIONS * BLOCK), POSITIONS * BLOCK, 0)
        group_rows = group_rows.reshape(POSITIONS, BLOCK, COLS)
        order_row = lax.dynamic_index_in_dim(block_order, group_id, 0, False)
        count_row = lax.dynamic_index_in_dim(counts, group_id, 0, False)
        sign_rows = lax.dynamic_index_in_dim(sign_bits, group_id, 0, False)
        mask_rows = lax.dynamic_index_in_dim(row_mask, group_id, 0, False)
        picked = jnp.take(group_rows, order_row, axis=0)
        sketch_blocks = mix_blocks(picked, mask_rows, sign_rows, walsh_sign_matrix)
        flat_rows = sketch_blocks.reshape(POSITIONS * KEEP, COLS)
        group_gram = jnp.dot(flat_rows.T.astype(jnp.float32), flat_rows.astype(jnp.float32), precision=lax.Precision.HIGHEST, preferred_element_type=jnp.float32) / float(POSITIONS * KEEP)
        run_ends = jnp.cumsum(count_row)
        offsets = run_ends - count_row
        held_slots = jnp.arange(MOST, dtype=jnp.int32)
        slot_index = jnp.minimum(offsets[:, None] + held_slots[None, :], POSITIONS - 1).astype(jnp.int32)
        live_slot = held_slots[None, :] < count_row[:, None]
        sketch_output = jnp.take(sketch_blocks, slot_index.reshape(-1), axis=0).reshape(N_DEV, MOST, KEEP, COLS)
        sketch_output = jnp.where(live_slot[:, :, None, None], sketch_output, jnp.zeros_like(sketch_output))
        return (sketch_output, group_gram)
    sketch_all, group_grams = lax.map(one_group, jnp.arange(N_GRP, dtype=jnp.int32))
    lower_groups = jnp.linalg.cholesky(group_grams)
    group_factor = jnp.swapaxes(lower_groups, -1, -2)
    mean_gram = jnp.sum(group_grams, axis=0) / float(N_GRP)
    factor = jnp.linalg.cholesky(mean_gram).T
    return (sketch_all.reshape(N_GRP * N_DEV * MOST * KEEP, COLS), group_factor, factor)
```

```python
import jax
import jax.numpy as jnp
from jax import lax
from jax.experimental import pallas as pl
from jax.experimental.pallas import tpu as pltpu
from jax.sharding import PartitionSpec as P

BLOCK = 128
KEEP = 32
PB = 128
BS = 16
STEP = 2
f32 = jnp.float32
bf16 = jnp.bfloat16


def split(x):
    high = x.astype(bf16)
    return high, (x - high.astype(f32)).astype(bf16)


def dg(a, b, ca=1, cb=0):
    return lax.dot_general(a, b, (((ca,), (cb,)), ((), ())), preferred_element_type=f32)


def dot3(a, b, ca=1, cb=0):
    return dg(a[0], b[0], ca, cb) + (dg(a[0], b[1], ca, cb) + dg(a[1], b[0], ca, cb))


def iota(shape, axis):
    return lax.broadcasted_iota(jnp.int32, shape, axis)


def mix_kernel(blocks_dev, devices, capacity, scale):
    def kernel(me_ref, order_ref, counts_ref, sign_ref, mask_ref, x_ref, slots_ref, gram_ref,
               places, targets, filled, transform, mixed, high, low, sem):
        step = pl.program_id(0)
        steps = pl.num_programs(0)
        positions = sign_ref.shape[0]
        columns = x_ref.shape[1]

        @pl.when(step == 0)
        def _():
            me = me_ref[0]
            for device in range(devices):
                filled[device] = 0

            def place(p, state):
                owner, end = state
                owner, end = lax.while_loop(
                    lambda s: p >= s[1],
                    lambda s: (s[0] + 1, s[1] + counts_ref[0, s[0] + 1]),
                    (owner, end),
                )
                block = order_ref[0, p] - me * blocks_dev

                @pl.when((block >= 0) & (block < blocks_dev))
                def _():
                    slot = filled[owner]
                    filled[owner] = slot + 1
                    places[block] = p
                    targets[block] = lax.bitwise_xor(owner, me) * capacity + slot

                return owner, end

            lax.fori_loop(0, positions, place, (jnp.int32(0), counts_ref[0, 0]))
            masks = jnp.concatenate(
                [mask_ref[pl.ds(places[b], 1), :] for b in range(blocks_dev)], axis=0
            )
            signs = jnp.concatenate(
                [sign_ref[pl.ds(places[b], 1), :] for b in range(blocks_dev)], axis=0
            )
            upper = (iota((BLOCK, BLOCK), 0) <= iota((BLOCK, BLOCK), 1)).astype(bf16)
            running = dg(masks.astype(f32).astype(bf16), upper)
            ranked = jnp.where(masks == 1, running, 0.0)
            common = iota((BLOCK, BLOCK), 0) & iota((BLOCK, BLOCK), 1)
            for shift_by in (4, 2, 1):
                common = common ^ (common >> shift_by)
            walsh = (1 - 2 * (common & 1)).astype(f32).astype(bf16)
            rank = (iota((KEEP, BLOCK), 0) + 1).astype(f32)
            select = jnp.concatenate(
                [(ranked[b : b + 1, :] == rank).astype(f32) for b in range(blocks_dev)], axis=0
            )
            kept = dg(select.astype(bf16), walsh)
            flips = (1 - 2 * signs).astype(f32)
            for b in range(blocks_dev):
                transform[b * KEEP : (b + 1) * KEEP, :] = (
                    kept[b * KEEP : (b + 1) * KEEP, :] * flips[b : b + 1, :]
                ).astype(bf16)

        for half in range(STEP):
            row = pl.multiple_of((step * STEP + half) * KEEP, KEEP)
            t = transform[pl.ds(row, KEEP), :]
            xh, xl = split(x_ref[half * BLOCK : (half + 1) * BLOCK, :])
            s = (dg(t, xh) + dg(t, xl)) * (float(BLOCK) ** -0.5)
            mixed[pl.ds(row, KEEP), :] = s
            sh, sl = split(s)
            high[pl.ds(row, KEEP), :] = sh
            low[pl.ds(row, KEEP), :] = sl
            pltpu.make_async_copy(
                mixed.at[pl.ds(row, KEEP), :], slots_ref.at[targets[step * STEP + half]], sem
            ).start()

        @pl.when(step == steps - 1)
        def _():
            at = 0
            for i in range(columns // PB):
                rows = slice(i * PB, (i + 1) * PB)
                a = (high[:, rows], low[:, rows])
                b = (high[:, i * PB :], low[:, i * PB :])
                g = dot3(a, b, 0, 0) * scale
                for j in range(columns // PB - i):
                    gram_ref[at : at + PB, :] = g[:, j * PB : (j + 1) * PB]
                    at += PB
            for b in range(blocks_dev):
                pltpu.make_async_copy(
                    mixed.at[0:KEEP, :], slots_ref.at[0], sem
                ).wait()

    return kernel


def mix(me, order, counts, signs, masks, matrix, devices, capacity):
    blocks_dev = matrix.shape[0] // BLOCK
    columns = matrix.shape[1]
    positions = signs.shape[0]
    panels = columns // PB
    packed = panels * (panels + 1) // 2 * PB
    smem = pl.BlockSpec(memory_space=pltpu.SMEM)
    whole = pl.BlockSpec((positions, BLOCK), lambda i: (0, 0))
    return pl.pallas_call(
        mix_kernel(blocks_dev, devices, capacity, 1.0 / float(positions * KEEP)),
        grid=(blocks_dev // STEP,),
        in_specs=[smem, smem, smem, whole, whole,
                  pl.BlockSpec((STEP * BLOCK, columns), lambda i: (i, 0))],
        out_specs=[pl.BlockSpec(memory_space=pl.ANY),
                   pl.BlockSpec((packed, PB), lambda i: (0, 0))],
        out_shape=[jax.ShapeDtypeStruct((devices * capacity, KEEP, columns), f32),
                   jax.ShapeDtypeStruct((packed, PB), f32)],
        scratch_shapes=[
            pltpu.SMEM((blocks_dev,), jnp.int32),
            pltpu.SMEM((blocks_dev,), jnp.int32),
            pltpu.SMEM((devices,), jnp.int32),
            pltpu.VMEM((blocks_dev * KEEP, BLOCK), bf16),
            pltpu.VMEM((blocks_dev * KEEP, columns), f32),
            pltpu.VMEM((blocks_dev * KEEP, columns), bf16),
            pltpu.VMEM((blocks_dev * KEEP, columns), bf16),
            pltpu.SemaphoreType.DMA,
        ],
        name="mix_gram",
    )(me, order, counts, signs, masks, matrix)


def assemble_kernel(blocks_dev, devices, capacity, most):
    def kernel(me_ref, order_ref, counts_ref, *refs):
        arrived = refs[:devices]
        out_ref, zeros, filled, sem = refs[devices:]
        me = me_ref[0]
        zeros[...] = jnp.zeros_like(zeros)
        offset = jnp.int32(0)
        for device in range(devices):
            filled[device] = 0
            offset = offset + jnp.where(device < me, counts_ref[0, device], 0)
        count = counts_ref[0, me]

        def fill(j, carry):
            @pl.when(j < count)
            def _():
                source = order_ref[0, jnp.minimum(offset + j, order_ref.shape[1] - 1)] // blocks_dev
                slot = filled[source]
                filled[source] = slot + 1
                shift = lax.bitwise_xor(source, me)
                for s in range(devices):
                    @pl.when(shift == s)
                    def _():
                        pltpu.make_async_copy(arrived[s].at[slot], out_ref.at[j], sem).start()

            @pl.when(j >= count)
            def _():
                pltpu.make_async_copy(zeros, out_ref.at[j], sem).start()

            return carry

        lax.fori_loop(0, most, fill, 0)

        def drain(j, carry):
            pltpu.make_async_copy(zeros, out_ref.at[j], sem).wait()
            return carry

        lax.fori_loop(0, most, drain, 0)

    return kernel


def assemble(me, order, counts, arrived, blocks_dev, capacity, most):
    devices = len(arrived)
    columns = arrived[0].shape[-1]
    smem = pl.BlockSpec(memory_space=pltpu.SMEM)
    anywhere = pl.BlockSpec(memory_space=pl.ANY)
    return pl.pallas_call(
        assemble_kernel(blocks_dev, devices, capacity, most),
        in_specs=[smem, smem, smem] + [anywhere] * devices,
        out_specs=anywhere,
        out_shape=jax.ShapeDtypeStruct((most, KEEP, columns), f32),
        scratch_shapes=[pltpu.VMEM((KEEP, columns), f32),
                        pltpu.SMEM((devices,), jnp.int32),
                        pltpu.SemaphoreType.DMA],
        name="assemble",
    )(me, order, counts, *arrived)


def chain(R, C, lanes, store):
    inverse = jnp.zeros((BS, PB), f32)
    for k in range(BS):
        pivot = C[k][k : k + 1, :]
        reciprocal = 1.0 / pivot
        others = jnp.where(lanes == k, 0.0, C[k])
        ck = others * reciprocal
        for j in range(k + 1, BS):
            if j == k + 1:
                C[j] = C[j] - (others * C[j][k : k + 1, :]) * reciprocal
            else:
                C[j] = C[j] - ck * C[j][k : k + 1, :]
        root = lax.rsqrt(pivot)
        for t in range(len(R)):
            row = R[t][k : k + 1, :]
            store(t, k, row * root)
            R[t] = R[t] - ck * row
        inverse = jnp.where(lanes == k, reciprocal, inverse)
    return [r * inverse for r in R]


def factor_in_place(A, U, Ds, Gs, Us, Ws, n):
    panels = n // PB
    inner = PB // BS
    lanes = iota((BS, PB), 0)
    eye = (iota((PB, PB), 0) == iota((PB, PB), 1)).astype(f32)
    keep = iota((PB, PB), 1) >= iota((PB, PB), 0)
    row_n = iota((PB, n), 0)
    lane_n = iota((PB, n), 1)
    Ds[...] = A[0:PB, 0:PB]

    def body(panel, first):
        c0 = pl.multiple_of(panel * PB, PB)
        if not first:
            p0 = pl.multiple_of((panel - 1) * PB, PB)
            urow = dot3(split(Ws[...]), split(A[pl.ds(p0, PB), :]))
            urow = jnp.where(lane_n >= row_n + p0, urow, 0.0)
            U[pl.ds(p0, PB), :] = urow
            U[pl.ds(p0, PB), pl.ds(p0, PB)] = Us[...]
            uf = split(urow)
        Gs[...] = eye
        R = [Ds[0:BS, :], Gs[0:BS, :]]
        for m in range(inner):
            r0 = m * BS
            C = [jnp.broadcast_to(R[0][:, r0 + j : r0 + j + 1], (BS, PB)) for j in range(BS)]
            if m < inner - 1:
                An = [Ds[r0 + BS : r0 + 2 * BS, :], Gs[r0 + BS : r0 + 2 * BS, :]]
                Ln = [jnp.broadcast_to(An[0][:, r0 + j : r0 + j + 1], (BS, PB)) for j in range(BS)]

            def store(t, k, v):
                (Us if t == 0 else Ws)[r0 + k : r0 + k + 1, :] = v

            Z = chain(R, C, lanes, store)
            if m < inner - 1:
                following = []
                for t in range(2):
                    acc = [None] * 4
                    for k in range(BS):
                        p = Ln[k] * Z[t][k : k + 1, :]
                        acc[k % 4] = p if acc[k % 4] is None else acc[k % 4] + p
                    following.append(An[t] - ((acc[0] + acc[1]) + (acc[2] + acc[3])))
                rr = r0 + 2 * BS
                if rr < PB:
                    zh, zl = split(jnp.concatenate(Z, axis=1))

                    def pad(z):
                        parts = [z, jnp.zeros((PB - (m + 1) * BS, 2 * PB), bf16)]
                        if m:
                            parts = [jnp.zeros((m * BS, 2 * PB), bf16)] + parts
                        return jnp.concatenate(parts, axis=0)

                    update = dot3(split(Ds[rr:PB, :]), (pad(zh), pad(zl)))
                    Ds[rr:PB, :] = Ds[rr:PB, :] - update[:, :PB]
                    Gs[rr:PB, :] = Gs[rr:PB, :] - update[:, PB:]
                R = following
            if not first and 0 < m < panels:
                s = m * PB
                a = (uf[0][:, s : s + PB], uf[1][:, s : s + PB])
                b = (uf[0][:, s:], uf[1][:, s:])
                A[s : s + PB, s:] = A[s : s + PB, s:] - dot3(a, b, 0, 0)
        Us[...] = jnp.where(keep, Us[...], 0.0)
        nx = pl.multiple_of(jnp.minimum(panel + 1, panels - 1) * PB, PB)
        un = split(dot3(split(Ws[...]), split(A[pl.ds(c0, PB), pl.ds(nx, PB)])))
        Ds[...] = A[pl.ds(nx, PB), pl.ds(nx, PB)] - dot3(un, un, 0, 0)

    body(jnp.int32(0), True)

    def loop(panel, carry):
        body(panel, False)
        return carry

    lax.fori_loop(1, panels, loop, 0)
    U[n - PB : n, 0 : n - PB] = jnp.zeros((PB, n - PB), f32)
    U[n - PB : n, n - PB : n] = Us[...]


def factor_kernel(n, devices):
    panels = n // PB
    rows_dev = n // devices

    def kernel(me_ref, ga, gb, ma, mb, out_ref, A, U, Ds, Gs, Us, Ws, sem):
        me = me_ref[0]
        half = ga.shape[0]

        def load(first, second):
            at = 0
            for i in range(panels):
                for j in range(i, panels):
                    lo, hi = at, at + PB
                    at = hi
                    for src, base in ((first, 0), (second, half)):
                        s, e = max(lo, base), min(hi, base + half)
                        if s < e:
                            pltpu.make_async_copy(
                                src.at[s - base : e - base, :],
                                A.at[i * PB + s - lo : i * PB + e - lo, j * PB : (j + 1) * PB],
                                sem,
                            ).start()

        @pl.when(me % 2 == 0)
        def _():
            load(ga, gb)

        @pl.when(me % 2 == 1)
        def _():
            load(ma, mb)

        for i in range(panels):
            if i:
                A[i * PB : (i + 1) * PB, 0 : i * PB] = jnp.zeros((PB, i * PB), f32)
        for i in range(panels):
            for j in range(i, panels):
                pltpu.make_async_copy(
                    ga.at[0:PB, :], A.at[i * PB : (i + 1) * PB, j * PB : (j + 1) * PB], sem
                ).wait()
        factor_in_place(A, U, Ds, Gs, Us, Ws, n)
        mine = pl.multiple_of(me * rows_dev, rows_dev)
        other = pl.multiple_of(lax.bitwise_xor(me, 1) * rows_dev, rows_dev)
        first = pltpu.make_async_copy(U.at[pl.ds(mine, rows_dev), :], out_ref.at[0], sem)
        second = pltpu.make_async_copy(U.at[pl.ds(other, rows_dev), :], out_ref.at[1], sem)
        first.start()
        second.start()
        first.wait()
        second.wait()

    return kernel


def cholesky_rows(me, ga, gb, ma, mb, n, devices):
    rows_dev = n // devices
    smem = pl.BlockSpec(memory_space=pltpu.SMEM)
    anywhere = pl.BlockSpec(memory_space=pl.ANY)
    return pl.pallas_call(
        factor_kernel(n, devices),
        in_specs=[smem] + [anywhere] * 4,
        out_specs=anywhere,
        out_shape=jax.ShapeDtypeStruct((2, rows_dev, n), f32),
        scratch_shapes=[pltpu.VMEM((n, n), f32), pltpu.VMEM((n, n), f32)]
        + [pltpu.VMEM((PB, PB), f32)] * 4
        + [pltpu.SemaphoreType.DMA],
        name="cholesky",
    )(me, ga, gb, ma, mb)


def exchange_sum(x, axis, perm, bit):
    rows = x.shape[0] // 2
    low, high = x[:rows], x[rows:]
    arrived = lax.ppermute(jnp.where(bit == 0, high, low), axis, perm)
    return jnp.where(bit == 0, low, high) + arrived


def exchange_join(x, axis, perm, bit):
    arrived = lax.ppermute(x, axis, perm)
    return jnp.concatenate([jnp.where(bit == 0, x, arrived), jnp.where(bit == 0, arrived, x)], axis=0)


def body(matrix, block_order, counts, sign_bits, row_mask):
    blocks_dev = matrix.shape[0] // BLOCK
    columns = matrix.shape[1]
    devices = lax.axis_size("dev")
    groups = lax.axis_size("grp")
    me = lax.axis_index("dev").astype(jnp.int32)
    grp = lax.axis_index("grp").astype(jnp.int32)
    most = 2 * blocks_dev
    capacity = max(1, most // devices)
    core = me & 1
    me_array = me.reshape(1)

    slots, gram = mix(me_array, block_order, counts, sign_bits[0], row_mask[0], matrix, devices, capacity)
    pair = [(d, d ^ 1) for d in range(devices)]

    gram = exchange_sum(gram, "dev", pair, core)
    bits = [b for b in range(1, devices.bit_length() - 1)]
    orders = list(zip(bits, reversed(bits)))
    perms = [[(d, d ^ (1 << (o[d & 1]))) for d in range(devices)] for o in orders]
    mine = [jnp.where(core == 0, (me >> o[0]) & 1, (me >> o[1]) & 1) for o in orders]
    for perm, bit in zip(perms, mine):
        gram = exchange_sum(gram, "dev", perm, bit)

    def gather(x):
        for perm, bit in reversed(list(zip(perms, mine))):
            x = exchange_join(x, "dev", perm, bit)
        return x

    mean = gram * (1.0 / float(groups))
    levels = range(groups.bit_length() - 1)
    for b in levels:
        mean = exchange_sum(mean, "grp", [(g, g ^ (1 << b)) for g in range(groups)], (grp >> b) & 1)
    for b in reversed(levels):
        mean = exchange_join(mean, "grp", [(g, g ^ (1 << b)) for g in range(groups)], (grp >> b) & 1)

    group_half = gather(gram)
    group_other = lax.ppermute(group_half, "dev", [(d, d ^ 1) for d in range(devices) if d & 1])
    mean_half = gather(mean)
    mean_other = lax.ppermute(mean_half, "dev", [(d, d ^ 1) for d in range(devices) if not d & 1])
    rows = cholesky_rows(me_array, group_half, group_other, mean_other, mean_half, columns, devices)
    theirs = lax.ppermute(rows[1], "dev", pair)
    group_factor = jnp.where(core == 0, rows[0], theirs)[None]
    factor = jnp.where(core == 0, theirs, rows[0])

    slots, _ = lax.optimization_barrier((slots, mean_half[0:8]))
    slots = slots.reshape(devices, capacity, KEEP, columns)
    arrived = [slots[0]] + [
        lax.ppermute(slots[s], "dev", [(d, d ^ s) for d in range(devices)]) for s in range(1, devices)
    ]
    sketch = assemble(me_array, block_order, counts, arrived, blocks_dev, capacity, most)
    return (sketch.reshape(most * KEEP, columns), group_factor, factor)


def solution(mesh):
    placed = (
        P(("grp", "dev"), None),
        P("grp", None),
        P("grp", None),
        P("grp", None, None),
        P("grp", None, None),
    )
    return jax.shard_map(
        body,
        mesh=mesh,
        in_specs=placed,
        out_specs=(P(("grp", "dev"), None), P("grp", "dev", None), P("dev", None)),
        check_vma=False,
    )
```
